32 devices in a mesh: groups: 2 (over x), seq: 16 (over z, y, core).
Axes of the slice: x: 2, y: 2, z: 4, core: 2. Of those that a mesh axis runs over, the one named last changes fastest.
Arguments:
- query_block: bfloat16 [512, 4096], P(('groups', 'seq')), parts along dimension 0, may hold values from -112 to 112
- cache_keys: bfloat16 [8192, 2048], P(('groups', 'seq')), parts along dimension 0, may hold values from -4 to 4
- stored_values: bfloat16 [8192, 2048], P(('groups', 'seq')), parts along dimension 0, may hold values from -6 to 6
- live_counts: int32 [32], P(('groups', 'seq')), parts along dimension 0, may hold values from 128 to 256
- first_position: int32 [2], P('groups'), parts along dimension 0, may hold values from 0 to 3840
- out_weight: bfloat16 [4096, 5376], P('seq'), may hold values from -0.09375 to 0.09375
Outputs:
- attended: bfloat16 [512, 5376], P(('groups', 'seq')), parts along dimension 0
The draws below stay inside these ranges and needn't reach their ends.
There are 2 independent parts, one for each index of `groups`. The reference program is written for one: setup_inputs(seed, part) draws one part's arguments, and reference() takes and returns one part's arrays. A program takes and returns all parts, laid end to end along the dimension named above; an argument that names none is the same for every part. Nothing has to cross between parts.
Inputs may be any that keep to these rules, and one draw needn't show every extreme that they name: `live_counts`: the live slots of a block are its first ones.
All inputs are finite; a program needn't handle non-finite values.
Results may differ from the reference program's by a relative error of at most 0.0058.
Values may be sent and summed in bfloat16 or wider, within the bound.
A program may use at most 64 MiB of HBM per device.

```python
import jax
import jax.numpy as jnp
from jax import lax

D = 5376
QUERY_HEADS = 32
KEY_VALUE_HEADS = 16
HEAD_SIZE = 128
K_DEV = 256
QUERIES = 256
SLOT_COUNT = 4096
N_SEQ = 16


def draw_pair(key):
    folded = jax.random.fold_in(key, 4242)
    key_sample = jax.random.fold_in(folded, 0)
    query_draw = jax.random.fold_in(folded, 1)
    pick_draw = jax.random.fold_in(folded, 2)
    sign_draw = jax.random.fold_in(folded, 4)
    cache_entries = jnp.clip(jax.random.normal(key_sample, (SLOT_COUNT, KEY_VALUE_HEADS * HEAD_SIZE), jnp.float32), -4.0, 4.0)
    queries = jnp.clip(3.0 * jax.random.normal(query_draw, (QUERIES, QUERY_HEADS * HEAD_SIZE), jnp.float32), -12.0, 12.0)
    signs = jnp.where(jax.random.bernoulli(sign_draw, 0.5, (KEY_VALUE_HEADS * HEAD_SIZE,)), 4.0, -4.0).astype(jnp.float32)
    cache_entries = cache_entries.at[0].set(signs)
    cache_entries = cache_entries.at[1].set(0.99 * signs)
    chosen = jax.random.permutation(pick_draw, QUERIES)[:3]
    targets = jnp.array([120.0, 200.0, 300.0], jnp.float32)
    strengths = targets * 168.0 ** 0.5 / (16.0 * HEAD_SIZE)
    keys_per_head = jnp.repeat(signs.reshape(KEY_VALUE_HEADS, HEAD_SIZE), QUERY_HEADS // KEY_VALUE_HEADS, axis=0).reshape(QUERY_HEADS * HEAD_SIZE)
    queries = queries.at[chosen].set(strengths[:, None] * keys_per_head[None, :])
    return (queries, cache_entries)


def draw_query_block(key, part):
    queries, cache_entries = draw_pair(key)
    return queries.astype(jnp.bfloat16)


def draw_cache_keys(key, part):
    queries, cache_entries = draw_pair(key)
    return cache_entries.astype(jnp.bfloat16)


def with_ends(entries, stream_key, low, high):
    longest = entries.shape.index(max(entries.shape))
    spots = []
    for shift in (0, 1):
        where = [jax.random.randint(jax.random.fold_in(stream_key, axis), (), 0, length) for axis, length in enumerate(entries.shape)]
        where[longest] = (where[longest] + shift) % entries.shape[longest]
        spots.append(tuple(where))
    return entries.at[spots[0]].set(low).at[spots[1]].set(high)


def steps_of(rng, dims, cuts, least, high):
    level = 1.0
    for position, parts in cuts:
        steps = jax.random.uniform(jax.random.fold_in(jax.random.fold_in(rng, 6), position), (parts,), jnp.float32, least / len(cuts), high / len(cuts))
        level = level * jnp.repeat(jnp.exp(steps), dims[position] // parts).reshape((-1,) + (1,) * (len(dims) - 1 - position))
    return level


def bell_draw(rng, dims, width, most, pieces=(), kind=jnp.bfloat16):
    factor_of = steps_of(rng, dims, pieces, -0.22, 0.18) if pieces else 1.0
    result = jax.random.normal(rng, dims, jnp.float32) * width * factor_of
    return jnp.minimum(jnp.maximum(result, -most), most).astype(kind)


def setup_inputs(seed: int = 0, part: int = 0) -> dict:
    streams_of = jax.random.split(jax.random.key(seed), 7)
    part_splits = jax.random.split(jax.random.fold_in(streams_of[6], part), 7)
    return {
        "query_block": draw_query_block(jax.random.fold_in(jax.random.fold_in(streams_of[6], part), 71), part),
        "cache_keys": draw_cache_keys(jax.random.fold_in(jax.random.fold_in(streams_of[6], part), 71), part),
        "stored_values": bell_draw(part_splits[2], (SLOT_COUNT, KEY_VALUE_HEADS * HEAD_SIZE), 1.0, 6.0, ((0, 16),)),
        "live_counts": with_ends(jax.random.randint(part_splits[3], (N_SEQ,), K_DEV // 2, K_DEV + 1), jax.random.fold_in(part_splits[3], 1), K_DEV // 2, K_DEV).astype(jnp.int32),
        "first_position": jax.random.randint(part_splits[4], (1,), 0, SLOT_COUNT - QUERIES + 1).astype(jnp.int32),
        "out_weight": bell_draw(streams_of[5], (QUERY_HEADS * HEAD_SIZE, D), (QUERY_HEADS * HEAD_SIZE) ** -0.5, 0.09375, ((0, 16),)),
    }


score_scale = 168.0 ** -0.5
masked_value = -1e30


def head_partial(query_cols, key_cols, value_cols, allowed, group_width):
    row_count = query_cols.shape[0]
    grouped = query_cols.reshape(row_count, group_width, HEAD_SIZE).astype(jnp.float32)
    scores = jnp.einsum("rgd,kd->grk", grouped, key_cols.astype(jnp.float32), precision=lax.Precision.HIGHEST) * score_scale
    row_best = jnp.max(jnp.where(allowed[None], scores, masked_value), axis=2)
    shifted = jnp.where(allowed[None], scores - row_best[:, :, None], -jnp.inf)
    weights = jnp.exp(shifted)
    weight_sum = jnp.sum(weights, axis=2)
    safe_total = jnp.where(weight_sum > 0, weight_sum, 1.0)
    rounded = lax.optimization_barrier(weights.astype(jnp.bfloat16)).astype(jnp.float32)
    weighted = jnp.einsum("grk,kd->grd", rounded, value_cols.astype(jnp.float32), precision=lax.Precision.HIGHEST)
    value_partial_sum = (weighted / safe_total[:, :, None]).astype(jnp.bfloat16)
    log_sum_exp = jnp.where(weight_sum > 0, row_best + jnp.log(safe_total), masked_value)
    return value_partial_sum, log_sum_exp


def source_partial(query_block, cache_keys, stored_values, live_counts, first_position, source):
    key_start = (source * K_DEV).astype(jnp.int32)
    key_rows = lax.dynamic_slice_in_dim(cache_keys, key_start, K_DEV, 0)
    value_rows = lax.dynamic_slice_in_dim(stored_values, key_start, K_DEV, 0)
    key_index = lax.iota(jnp.int32, K_DEV)
    query_pos = first_position[0] + lax.iota(jnp.int32, QUERIES)
    allowed = (key_index[None, :] < live_counts[source]) & (key_start + key_index[None, :] <= query_pos[:, None])
    group_width = QUERY_HEADS // KEY_VALUE_HEADS
    partial_list = []
    logsum_list = []
    for key_value_head in range(KEY_VALUE_HEADS):
        query_cols = query_block[:, key_value_head * group_width * HEAD_SIZE:(key_value_head + 1) * group_width * HEAD_SIZE]
        key_cols = key_rows[:, key_value_head * HEAD_SIZE:(key_value_head + 1) * HEAD_SIZE]
        value_cols = value_rows[:, key_value_head * HEAD_SIZE:(key_value_head + 1) * HEAD_SIZE]
        value_partial_sum, log_sum_exp = head_partial(query_cols, key_cols, value_cols, allowed, group_width)
        partial_list.append(value_partial_sum)
        logsum_list.append(log_sum_exp)
    value_partial_sum = jnp.transpose(jnp.stack(partial_list), (2, 0, 1, 3)).reshape(QUERIES, QUERY_HEADS, HEAD_SIZE)
    log_sum_exp = jnp.transpose(jnp.stack(logsum_list), (2, 0, 1)).reshape(QUERIES, QUERY_HEADS)
    return value_partial_sum, log_sum_exp


def reference(query_block, cache_keys, stored_values, live_counts, first_position, out_weight):
    def one_source(source):
        return source_partial(query_block, cache_keys, stored_values, live_counts, first_position, source)

    partials, logsums = lax.map(one_source, jnp.arange(N_SEQ, dtype=jnp.int32))
    largest = jnp.max(logsums, axis=0)
    scales = jnp.exp(logsums - largest[None])
    merged = (jnp.sum(scales[..., None] * partials.astype(jnp.float32), axis=0) / jnp.sum(scales, axis=0)[..., None]).astype(jnp.bfloat16)
    per_group = QUERY_HEADS // N_SEQ
    flattened = merged.reshape(QUERIES, QUERY_HEADS * HEAD_SIZE)

    def add_group(group, running):
        offset = (group * (per_group * HEAD_SIZE)).astype(jnp.int32)
        head_columns = lax.dynamic_slice_in_dim(flattened, offset, per_group * HEAD_SIZE, 1)
        weight_rows = lax.dynamic_slice_in_dim(out_weight, offset, per_group * HEAD_SIZE, 0)
        projected = jnp.dot(head_columns, weight_rows, preferred_element_type=jnp.float32)
        return running + projected

    summed = lax.fori_loop(jnp.int32(0), jnp.int32(N_SEQ), add_group, jnp.zeros((QUERIES, D), jnp.float32))
    return summed.astype(jnp.bfloat16)
```

```python
import functools

import jax
import jax.numpy as jnp
from jax import lax
from jax.experimental import pallas as pl
from jax.experimental.pallas import tpu as pltpu
from jax.sharding import PartitionSpec as P

QUERY_HEADS = 32
KEY_VALUE_HEADS = 16
HEAD_SIZE = 128

score_scale = 168.0 ** (-0.5)
masked_value = -1e30
MESH = pl.DeviceIdType.MESH


def bit_of(index, bit):
    return (index // (1 << bit)) % 2


def flipped(index, mask):
    result = index
    bit = 0
    while (1 << bit) <= mask:
        if (mask >> bit) & 1:
            result = result + (1 - 2 * bit_of(index, bit)) * (1 << bit)
        bit += 1
    return result


def place_of(dest, order):
    place = 0
    for step, bit in enumerate(order):
        place = place + bit_of(dest, bit) * (1 << (len(order) - 1 - step))
    return place


def dest_at(place, order):
    dest = 0
    for step, bit in enumerate(order):
        dest = dest + bit_of(place, len(order) - 1 - step) * (1 << bit)
    return dest


def kernel(
    n, q_ref, live_ref, first_ref, k_hbm, v_hbm, w_hbm, out_ref,
    q_all, k_buf, v_buf, w_buf, part_a, part_b, lse_a, lse_b, got_a, got_b, gotl_a, gotl_b,
    acc, sent, came,
    load_sem, q_send, q_recv, p_send, p_recv, t_send, t_recv,
):
    me = lax.axis_index("seq")
    bits = n.bit_length() - 1
    orders = (list(range(bits)), [0] + list(range(2, bits)) + [1])
    per_dest = QUERY_HEADS // n
    group_width = QUERY_HEADS // KEY_VALUE_HEADS
    key_count = k_buf.shape[0]
    rows_each = q_ref.shape[1]
    rows = rows_each * n
    half_rows = rows // 2
    half_cols = q_ref.shape[2] // 2
    out_half = out_ref.shape[1] // 2
    parts, lses = (part_a, part_b), (lse_a, lse_b)
    gots, gotls = (got_a, got_b), (gotl_a, gotl_b)

    loads = [
        pltpu.make_async_copy(src, dst, load_sem.at[i])
        for i, (src, dst) in enumerate(((k_hbm, k_buf), (v_hbm, v_buf), (w_hbm, w_buf)))
    ]
    for load in loads:
        load.start()
    own = pltpu.make_async_copy(q_ref.at[0], q_all.at[me], load_sem.at[3])
    own.start()

    barrier = pltpu.get_barrier_semaphore()
    for bit in range(bits):
        pl.semaphore_signal(
            barrier, inc=1, device_id={"seq": flipped(me, 1 << bit)}, device_id_type=MESH
        )
    pl.semaphore_wait(barrier, bits)

    def q_copy(c, held, bit):
        cols = pl.ds(c * half_cols, half_cols)
        block = flipped(me, held)
        mask = held | (1 << bit)
        src = q_ref.at[0, :, cols] if held == 0 else q_all.at[block, :, cols]
        return pltpu.make_async_remote_copy(
            src_ref=src,
            dst_ref=q_all.at[block, :, cols],
            send_sem=q_send.at[c, mask],
            recv_sem=q_recv.at[c, mask],
            device_id={"seq": flipped(me, 1 << bit)},
            device_id_type=MESH,
        )

    def q_arrival(c, mask):
        cols = pl.ds(c * half_cols, half_cols)
        block = flipped(me, mask)
        return pltpu.make_async_remote_copy(
            src_ref=q_all.at[block, :, cols],
            dst_ref=q_all.at[block, :, cols],
            send_sem=q_send.at[c, mask],
            recv_sem=q_recv.at[c, mask],
            device_id={"seq": flipped(me, 1)},
            device_id_type=MESH,
        )

    walks = [[b for b in reversed(order) if b != 0] for order in orders]
    held = [[0], [0]]
    q_copies = []
    for step in range(bits - 1):
        for c in range(2):
            for mask in held[c]:
                copy = q_copy(c, mask, walks[c][step])
                copy.start()
                q_copies.append(copy)
        if step == 0:
            for c in range(2):
                copy = q_copy(c, 0, 0)
                copy.start()
                q_copies.append(copy)
        for c in range(2):
            new = [mask | (1 << walks[c][step]) for mask in held[c]]
            for mask in new:
                q_arrival(c, mask).wait_recv()
                copy = q_copy(c, mask, 0)
                copy.start()
                q_copies.append(copy)
            held[c] = held[c] + new
    for c in range(2):
        for mask in held[c]:
            q_arrival(c, mask | 1).wait_recv()
    own.wait()
    loads[0].wait()
    loads[1].wait()

    slot = lax.broadcasted_iota(jnp.int32, (key_count, rows), 0)
    row = lax.broadcasted_iota(jnp.int32, (key_count, rows), 1)
    allowed = (slot < live_ref[0]) & (me * key_count + slot <= first_ref[0] + row)

    def attend(i, start):
        place = start + i
        dest = dest_at(place // per_dest, orders[0])
        head = dest * per_dest + place % per_dest
        key_head = head // group_width
        q = q_all[:, :, pl.ds(pl.multiple_of(head * HEAD_SIZE, HEAD_SIZE), HEAD_SIZE)]
        q = q.reshape(rows, HEAD_SIZE)
        kv_cols = pl.ds(pl.multiple_of(key_head * HEAD_SIZE, HEAD_SIZE), HEAD_SIZE)
        scores = lax.dot_general(
            k_buf[:, kv_cols], q, (((1,), (1,)), ((), ())), preferred_element_type=jnp.float32
        ) * score_scale
        scores = jnp.where(allowed, scores, masked_value)
        best = jnp.max(scores, axis=0, keepdims=True)
        weights = jnp.where(allowed, jnp.exp(scores - best), 0.0)
        total = jnp.sum(weights, axis=0, keepdims=True)
        safe = jnp.where(total > 0, total, 1.0)
        weighted = lax.dot_general(
            v_buf[:, kv_cols], weights.astype(jnp.bfloat16), (((0,), (0,)), ((), ())),
            preferred_element_type=jnp.float32,
        )
        partial = (weighted * (1.0 / safe)).astype(jnp.bfloat16)
        lse = jnp.where(total > 0, best + jnp.log(safe), masked_value)
        for c in range(2):
            at = place_of(dest, orders[c]) * per_dest + place % per_dest
            parts[c][at] = partial[:, c * half_rows:(c + 1) * half_rows]
            lses[c][at] = lse[:, c * half_rows:(c + 1) * half_rows]
        return start

    def spans(c, step):
        base = 0
        for earlier in range(step):
            base = base + bit_of(me, orders[c][earlier]) * (n >> (earlier + 1))
        size = n >> (step + 1)
        mine = bit_of(me, orders[c][step])
        return base + (1 - mine) * size, base + mine * size, n - 2 * size, size

    def p_copies(c, step):
        away, _, landing, size = spans(c, step)
        src = pl.ds(away * per_dest, size * per_dest)
        dst = pl.ds(landing * per_dest, size * per_dest)
        return [
            pltpu.make_async_remote_copy(
                src_ref=source.at[src],
                dst_ref=target.at[dst],
                send_sem=p_send.at[c, step, i],
                recv_sem=p_recv.at[c, step, i],
                device_id={"seq": flipped(me, 1 << orders[c][step])},
                device_id_type=MESH,
            )
            for i, (source, target) in enumerate(((parts[c], gots[c]), (lses[c], gotls[c])))
        ]

    def merge(c, start, landing, count):
        def one(i, carry):
            at, came_at = start + i, landing + i
            left, right = lses[c][at], gotls[c][came_at]
            top = jnp.maximum(left, right)
            scale_l, scale_r = jnp.exp(left - top), jnp.exp(right - top)
            whole = scale_l + scale_r
            inverse = 1.0 / whole
            mixed = parts[c][at].astype(jnp.float32) * (scale_l * inverse) + gots[c][
                came_at
            ].astype(jnp.float32) * (scale_r * inverse)
            parts[c][at] = mixed.astype(jnp.bfloat16)
            lses[c][at] = top + jnp.log(whole)
            return carry

        lax.fori_loop(0, count, one, 0)

    half_heads = QUERY_HEADS // 2
    away0, keep0, _, _ = spans(0, 0)
    lax.fori_loop(0, half_heads, attend, away0 * per_dest)
    pending = []
    flying = [p_copies(c, 0) for c in range(2)]
    for copies in flying:
        for copy in copies:
            copy.start()
    lax.fori_loop(0, half_heads, attend, keep0 * per_dest)
    for step in range(bits):
        for c in range(2):
            _, keep, landing, size = spans(c, step)
            for copy in flying[c]:
                copy.wait_recv()
            pending += flying[c]
            merge(c, keep * per_dest, landing * per_dest, size * per_dest)
            if step + 1 < bits:
                flying[c] = p_copies(c, step + 1)
                for copy in flying[c]:
                    copy.start()

    loads[2].wait()
    merged = []
    for c in range(2):
        at = place_of(me, orders[c]) * per_dest
        merged.append(parts[c][pl.ds(at, per_dest)].reshape(per_dest * HEAD_SIZE, half_rows))

    def t_copy(c, step):
        away, _, landing, size = spans(c, step)
        return pltpu.make_async_remote_copy(
            src_ref=sent.at[c, pl.ds(away, size)],
            dst_ref=came.at[c, pl.ds(landing, size)],
            send_sem=t_send.at[c, step],
            recv_sem=t_recv.at[c, step],
            device_id={"seq": flipped(me, 1 << orders[c][step])},
            device_id_type=MESH,
        )

    def ship(c, step):
        away, _, _, size = spans(c, step)

        def one(i, carry):
            sent[c, away + i] = acc[c, away + i].astype(jnp.bfloat16)
            return carry

        lax.fori_loop(0, size, one, 0)
        copy = t_copy(c, step)
        copy.start()
        return copy

    flying = []
    for c in range(2):
        for r in range(2):
            term = lax.dot_general(
                merged[r], w_buf[:, c * out_half:(c + 1) * out_half], (((0,), (0,)), ((), ())),
                preferred_element_type=jnp.float32,
            )
            for j in range(n // 2):
                at = place_of(r * (n // 2) + j, orders[c])
                acc[c, at] = term[j * rows_each:(j + 1) * rows_each]
        flying.append(ship(c, 0))
    for step in range(bits):
        for c in range(2):
            _, keep, landing, size = spans(c, step)
            flying[c].wait_recv()
            pending.append(flying[c])

            def add(i, carry):
                acc[c, keep + i] = acc[c, keep + i] + came[c, landing + i].astype(jnp.float32)
                return carry

            lax.fori_loop(0, size, add, 0)
            if step + 1 < bits:
                flying[c] = ship(c, step + 1)
    for c in range(2):
        at = place_of(me, orders[c])
        out_ref[:, c * out_half:(c + 1) * out_half] = acc[c, at].astype(jnp.bfloat16)
    for copy in q_copies + pending:
        copy.wait_send()


def body(query_block, cache_keys, stored_values, live_counts, first_position, out_weight):
    n = lax.axis_size("seq")
    bits = n.bit_length() - 1
    rows_each, width = query_block.shape
    half_rows = rows_each * n // 2
    d_model = out_weight.shape[1]
    per_dest = QUERY_HEADS // n
    vmem = pl.BlockSpec(memory_space=pltpu.VMEM)
    smem = pl.BlockSpec(memory_space=pltpu.SMEM)
    anywhere = pl.BlockSpec(memory_space=pl.ANY)
    bf16, f32 = jnp.bfloat16, jnp.float32
    dma = pltpu.SemaphoreType.DMA
    return pl.pallas_call(
        functools.partial(kernel, n),
        out_shape=jax.ShapeDtypeStruct((rows_each, d_model), bf16),
        in_specs=[vmem, smem, smem, anywhere, anywhere, anywhere],
        out_specs=vmem,
        scratch_shapes=[
            pltpu.VMEM((n, rows_each, width), bf16),
            pltpu.VMEM(cache_keys.shape, bf16),
            pltpu.VMEM(stored_values.shape, bf16),
            pltpu.VMEM(out_weight.shape, bf16),
            pltpu.VMEM((QUERY_HEADS, HEAD_SIZE, half_rows), bf16),
            pltpu.VMEM((QUERY_HEADS, HEAD_SIZE, half_rows), bf16),
            pltpu.VMEM((QUERY_HEADS, 1, half_rows), f32),
            pltpu.VMEM((QUERY_HEADS, 1, half_rows), f32),
            pltpu.VMEM((QUERY_HEADS, HEAD_SIZE, half_rows), bf16),
            pltpu.VMEM((QUERY_HEADS, HEAD_SIZE, half_rows), bf16),
            pltpu.VMEM((QUERY_HEADS, 1, half_rows), f32),
            pltpu.VMEM((QUERY_HEADS, 1, half_rows), f32),
            pltpu.VMEM((2, n, rows_each, d_model // 2), f32),
            pltpu.VMEM((2, n, rows_each, d_model // 2), bf16),
            pltpu.VMEM((2, n, rows_each, d_model // 2), bf16),
            dma((4,)),
            dma((2, n)),
            dma((2, n)),
            dma((2, bits, 2)),
            dma((2, bits, 2)),
            dma((2, bits)),
            dma((2, bits)),
        ],
        compiler_params=pltpu.CompilerParams(
            collective_id=0, has_side_effects=True, vmem_limit_bytes=48 * 1024 * 1024
        ),
        name="attend_project",
    )(query_block[None], live_counts, first_position, cache_keys, stored_values, out_weight)


def solution(mesh):
    in_specs = (
        P(("groups", "seq"), None),
        P(("groups", "seq"), None),
        P(("groups", "seq"), None),
        P(("groups", "seq")),
        P("groups"),
        P("seq", None),
    )
    out_specs = P(("groups", "seq"), None)
    return jax.shard_map(body, mesh=mesh, in_specs=in_specs, out_specs=out_specs, check_vma=False)
```

```python
import functools

import jax
import jax.numpy as jnp
from jax import lax
from jax.experimental import pallas as pl
from jax.experimental.pallas import tpu as pltpu
from jax.sharding import PartitionSpec as P

QUERY_HEADS = 32
KEY_VALUE_HEADS = 16
HEAD_SIZE = 128

score_scale = 168.0 ** (-0.5)
masked_value = -1e30
MESH = pl.DeviceIdType.MESH


def bit_of(index, bit):
    return (index // (1 << bit)) % 2


def flipped(index, mask):
    result = index
    bit = 0
    while (1 << bit) <= mask:
        if (mask >> bit) & 1:
            result = result + (1 - 2 * bit_of(index, bit)) * (1 << bit)
        bit += 1
    return result


def place_of(dest, order):
    place = 0
    for step, bit in enumerate(order):
        place = place + bit_of(dest, bit) * (1 << (len(order) - 1 - step))
    return place


def dest_at(place, order):
    dest = 0
    for step, bit in enumerate(order):
        dest = dest + bit_of(place, len(order) - 1 - step) * (1 << bit)
    return dest


def kernel(
    n, q_ref, live_ref, first_ref, k_hbm, v_hbm, w_hbm, out_ref,
    q_all, k_buf, v_buf, w_buf, parts, lses, gots, gotls, acc, sent, came,
    load_sem, q_send, q_recv, p_send, p_recv, t_send, t_recv,
):
    me = lax.axis_index("seq")
    bits = n.bit_length() - 1
    orders = (list(range(bits)), [0] + list(range(2, bits)) + [1])
    per_dest = QUERY_HEADS // n
    group_width = QUERY_HEADS // KEY_VALUE_HEADS
    key_count = k_buf.shape[0]
    rows_each = q_ref.shape[1]
    rows = rows_each * n
    half_rows = rows // 2
    half_cols = q_ref.shape[2] // 2
    p_flows = parts.shape[0]
    t_flows, out_part = acc.shape[0], acc.shape[3]

    loads = [
        pltpu.make_async_copy(src, dst, load_sem.at[i])
        for i, (src, dst) in enumerate(((k_hbm, k_buf), (v_hbm, v_buf), (w_hbm, w_buf)))
    ]
    for load in loads:
        load.start()
    own = pltpu.make_async_copy(q_ref.at[0], q_all.at[me], load_sem.at[3])
    own.start()

    barrier = pltpu.get_barrier_semaphore()
    for bit in range(bits):
        pl.semaphore_signal(
            barrier, inc=1, device_id={"seq": flipped(me, 1 << bit)}, device_id_type=MESH
        )
    pl.semaphore_wait(barrier, bits)

    def q_copy(c, held, bit):
        cols = pl.ds(c * half_cols, half_cols)
        block = flipped(me, held)
        mask = held | (1 << bit)
        src = q_ref.at[0, :, cols] if held == 0 else q_all.at[block, :, cols]
        return pltpu.make_async_remote_copy(
            src_ref=src,
            dst_ref=q_all.at[block, :, cols],
            send_sem=q_send.at[c, mask],
            recv_sem=q_recv.at[c, mask],
            device_id={"seq": flipped(me, 1 << bit)},
            device_id_type=MESH,
        )

    def q_arrival(c, mask):
        cols = pl.ds(c * half_cols, half_cols)
        block = flipped(me, mask)
        return pltpu.make_async_remote_copy(
            src_ref=q_all.at[block, :, cols],
            dst_ref=q_all.at[block, :, cols],
            send_sem=q_send.at[c, mask],
            recv_sem=q_recv.at[c, mask],
            device_id={"seq": flipped(me, 1)},
            device_id_type=MESH,
        )

    walks = [[b for b in reversed(order) if b != 0] for order in orders]
    held = [[0], [0]]
    q_copies = []
    for step in range(bits - 1):
        for c in range(2):
            for mask in held[c]:
                copy = q_copy(c, mask, walks[c][step])
                copy.start()
                q_copies.append(copy)
        if step == 0:
            for c in range(2):
                copy = q_copy(c, 0, 0)
                copy.start()
                q_copies.append(copy)
        for c in range(2):
            new = [mask | (1 << walks[c][step]) for mask in held[c]]
            for mask in new:
                q_arrival(c, mask).wait_recv()
                copy = q_copy(c, mask, 0)
                copy.start()
                q_copies.append(copy)
            held[c] = held[c] + new
    for c in range(2):
        for mask in held[c]:
            q_arrival(c, mask | 1).wait_recv()
    own.wait()
    loads[0].wait()
    loads[1].wait()

    slot = lax.broadcasted_iota(jnp.int32, (key_count, rows), 0)
    row = lax.broadcasted_iota(jnp.int32, (key_count, rows), 1)
    allowed = (slot < live_ref[0]) & (me * key_count + slot <= first_ref[0] + row)

    def attend(sub, i, start):
        dest = dest_at(start + i, orders[0])
        head = dest * per_dest + sub
        key_head = head // group_width
        q = q_all[:, :, pl.ds(pl.multiple_of(head * HEAD_SIZE, HEAD_SIZE), HEAD_SIZE)]
        q = q.reshape(rows, HEAD_SIZE)
        kv_cols = pl.ds(pl.multiple_of(key_head * HEAD_SIZE, HEAD_SIZE), HEAD_SIZE)
        scores = lax.dot_general(
            k_buf[:, kv_cols], q, (((1,), (1,)), ((), ())), preferred_element_type=jnp.float32
        ) * score_scale
        scores = jnp.where(allowed, scores, masked_value)
        best = jnp.max(scores, axis=0, keepdims=True)
        weights = jnp.where(allowed, jnp.exp(scores - best), 0.0)
        total = jnp.sum(weights, axis=0, keepdims=True)
        safe = jnp.where(total > 0, total, 1.0)
        weighted = lax.dot_general(
            v_buf[:, kv_cols], weights.astype(jnp.bfloat16), (((0,), (0,)), ((), ())),
            preferred_element_type=jnp.float32,
        )
        partial = (weighted * (1.0 / safe)).astype(jnp.bfloat16)
        lse = jnp.where(total > 0, best + jnp.log(safe), masked_value)
        for c in range(2):
            at = place_of(dest, orders[c])
            parts[2 * sub + c, at] = partial[:, c * half_rows:(c + 1) * half_rows]
            lses[2 * sub + c, at] = lse[:, c * half_rows:(c + 1) * half_rows]
        return start

    def spans(c, step):
        base = 0
        for earlier in range(step):
            base = base + bit_of(me, orders[c][earlier]) * (n >> (earlier + 1))
        size = n >> (step + 1)
        mine = bit_of(me, orders[c][step])
        return base + (1 - mine) * size, base + mine * size, n - 2 * size, size

    def p_copies(f, step):
        away, _, landing, size = spans(f % 2, step)
        return [
            pltpu.make_async_remote_copy(
                src_ref=source.at[f, pl.ds(away, size)],
                dst_ref=target.at[f, pl.ds(landing, size)],
                send_sem=p_send.at[f, step, i],
                recv_sem=p_recv.at[f, step, i],
                device_id={"seq": flipped(me, 1 << orders[f % 2][step])},
                device_id_type=MESH,
            )
            for i, (source, target) in enumerate(((parts, gots), (lses, gotls)))
        ]

    def merge(f, start, landing, count):
        def one(i, carry):
            at, came_at = start + i, landing + i
            left, right = lses[f, at], gotls[f, came_at]
            top = jnp.maximum(left, right)
            scale_l, scale_r = jnp.exp(left - top), jnp.exp(right - top)
            whole = scale_l + scale_r
            inverse = 1.0 / whole
            mixed = parts[f, at].astype(jnp.float32) * (scale_l * inverse) + gots[
                f, came_at
            ].astype(jnp.float32) * (scale_r * inverse)
            parts[f, at] = mixed.astype(jnp.bfloat16)
            lses[f, at] = top + jnp.log(whole)
            return carry

        lax.fori_loop(0, count, one, 0, unroll=min(count, 4))

    pending = []
    flying = {}

    def p_start(f, step):
        flying[f] = p_copies(f, step)
        for copy in flying[f]:
            copy.start()

    def p_turn(f, step):
        _, keep, landing, size = spans(f % 2, step)
        for copy in flying[f]:
            copy.wait_recv()
        pending.extend(flying[f])
        merge(f, keep, landing, size)
        if step + 1 < bits:
            p_start(f, step + 1)

    away0, keep0, _, _ = spans(0, 0)
    for sub in range(per_dest):
        lax.fori_loop(0, n // 2, functools.partial(attend, sub), away0, unroll=4)
        p_start(2 * sub, 0)
        p_start(2 * sub + 1, 0)
    for sub in range(per_dest):
        lax.fori_loop(0, n // 2, functools.partial(attend, sub), keep0, unroll=4)
        p_turn(2 * sub, 0)
        p_turn(2 * sub + 1, 0)
    for step in range(1, bits):
        for f in range(p_flows):
            p_turn(f, step)

    loads[2].wait()
    merged = []
    for c in range(2):
        at = place_of(me, orders[c])
        merged.append(
            jnp.concatenate([parts[2 * sub + c, at] for sub in range(per_dest)], axis=0)
        )

    def t_copy(f, step):
        away, _, landing, size = spans(f % 2, step)
        return pltpu.make_async_remote_copy(
            src_ref=sent.at[f, pl.ds(away, size)],
            dst_ref=came.at[f, pl.ds(landing, size)],
            send_sem=t_send.at[f, step],
            recv_sem=t_recv.at[f, step],
            device_id={"seq": flipped(me, 1 << orders[f % 2][step])},
            device_id_type=MESH,
        )

    def ship(f, step):
        away, _, _, size = spans(f % 2, step)

        def one(i, carry):
            sent[f, away + i] = acc[f, away + i].astype(jnp.bfloat16)
            return carry

        lax.fori_loop(0, size, one, 0, unroll=min(size, 4))
        copy = t_copy(f, step)
        copy.start()
        return copy

    flying = []
    for f in range(t_flows):
        for r in range(2):
            term = lax.dot_general(
                merged[r], w_buf[:, f * out_part:(f + 1) * out_part], (((0,), (0,)), ((), ())),
                preferred_element_type=jnp.float32,
            )
            for j in range(n // 2):
                at = place_of(r * (n // 2) + j, orders[f % 2])
                acc[f, at] = term[j * rows_each:(j + 1) * rows_each]
        flying.append(ship(f, 0))
    for step in range(bits):
        for f in range(t_flows):
            _, keep, landing, size = spans(f % 2, step)
            flying[f].wait_recv()
            pending.append(flying[f])

            def add(i, carry):
                acc[f, keep + i] = acc[f, keep + i] + came[f, landing + i].astype(jnp.float32)
                return carry

            lax.fori_loop(0, size, add, 0, unroll=min(size, 4))
            if step + 1 < bits:
                flying[f] = ship(f, step + 1)
    for f in range(t_flows):
        at = place_of(me, orders[f % 2])
        out_ref[:, f * out_part:(f + 1) * out_part] = acc[f, at].astype(jnp.bfloat16)
    for copy in q_copies + pending:
        copy.wait_send()


def body(query_block, cache_keys, stored_values, live_counts, first_position, out_weight):
    n = lax.axis_size("seq")
    bits = n.bit_length() - 1
    rows_each, width = query_block.shape
    half_rows = rows_each * n // 2
    d_model = out_weight.shape[1]
    per_dest = QUERY_HEADS // n
    p_flows = 2 * per_dest
    t_flows = max(f for f in (2, 4, 6) if d_model % (128 * f) == 0)
    vmem = pl.BlockSpec(memory_space=pltpu.VMEM)
    smem = pl.BlockSpec(memory_space=pltpu.SMEM)
    anywhere = pl.BlockSpec(memory_space=pl.ANY)
    bf16, f32 = jnp.bfloat16, jnp.float32
    dma = pltpu.SemaphoreType.DMA
    return pl.pallas_call(
        functools.partial(kernel, n),
        out_shape=jax.ShapeDtypeStruct((rows_each, d_model), bf16),
        in_specs=[anywhere, smem, smem, anywhere, anywhere, anywhere],
        out_specs=vmem,
        scratch_shapes=[
            pltpu.VMEM((n, rows_each, width), bf16),
            pltpu.VMEM(cache_keys.shape, bf16),
            pltpu.VMEM(stored_values.shape, bf16),
            pltpu.VMEM(out_weight.shape, bf16),
            pltpu.VMEM((p_flows, n, HEAD_SIZE, half_rows), bf16),
            pltpu.VMEM((p_flows, n, 1, half_rows), f32),
            pltpu.VMEM((p_flows, n, HEAD_SIZE, half_rows), bf16),
            pltpu.VMEM((p_flows, n, 1, half_rows), f32),
            pltpu.VMEM((t_flows, n, rows_each, d_model // t_flows), f32),
            pltpu.VMEM((t_flows, n, rows_each, d_model // t_flows), bf16),
            pltpu.VMEM((t_flows, n, rows_each, d_model // t_flows), bf16),
            dma((4,)),
            dma((2, n)),
            dma((2, n)),
            dma((p_flows, bits, 2)),
            dma((p_flows, bits, 2)),
            dma((t_flows, bits)),
            dma((t_flows, bits)),
        ],
        compiler_params=pltpu.CompilerParams(
            collective_id=0, has_side_effects=True, vmem_limit_bytes=63 * 1024 * 1024
        ),
        name="attend_project",
    )(query_block[None], live_counts, first_position, cache_keys, stored_values, out_weight)


def solution(mesh):
    in_specs = (
        P(("groups", "seq"), None),
        P(("groups", "seq"), None),
        P(("groups", "seq"), None),
        P(("groups", "seq")),
        P("groups"),
        P("seq", None),
    )
    out_specs = P(("groups", "seq"), None)
    return jax.shard_map(body, mesh=mesh, in_specs=in_specs, out_specs=out_specs, check_vma=False)
```

```python
import functools

import jax
import jax.numpy as jnp
from jax import lax
from jax.experimental import pallas as pl
from jax.experimental.pallas import tpu as pltpu
from jax.sharding import PartitionSpec as P

QUERY_HEADS = 32
KEY_VALUE_HEADS = 16
HEAD_SIZE = 128

score_scale = 168.0 ** (-0.5)
masked_value = -1e30
MESH = pl.DeviceIdType.MESH


def bit_of(index, bit):
    return (index // (1 << bit)) % 2


def flipped(index, mask):
    result = index
    bit = 0
    while (1 << bit) <= mask:
        if (mask >> bit) & 1:
            result = result + (1 - 2 * bit_of(index, bit)) * (1 << bit)
        bit += 1
    return result


def place_of(dest, order):
    place = 0
    for step, bit in enumerate(order):
        place = place + bit_of(dest, bit) * (1 << (len(order) - 1 - step))
    return place


def dest_at(place, order):
    dest = 0
    for step, bit in enumerate(order):
        dest = dest + bit_of(place, len(order) - 1 - step) * (1 << bit)
    return dest


def kernel(
    n, q_ref, live_ref, first_ref, k_hbm, v_hbm, w_hbm, out_ref,
    q_all, k_buf, v_buf, w_buf, parts, lses, gots, gotls, acc, sent, came,
    load_sem, own_sem, q_send, q_recv, p_send, p_recv, t_send, t_recv,
):
    me = lax.axis_index("seq")
    bits = n.bit_length() - 1
    orders = (list(range(bits)), [0] + list(range(2, bits)) + [1])
    per_dest = QUERY_HEADS // n
    group_width = QUERY_HEADS // KEY_VALUE_HEADS
    key_count = k_buf.shape[0]
    rows_each = q_ref.shape[1]
    rows = rows_each * n
    half_rows = rows // 2
    half_dests = n // 2
    p_flows = parts.shape[0]
    t_flows, out_part = acc.shape[0], acc.shape[3]

    loads = [
        pltpu.make_async_copy(src, dst, load_sem.at[i])
        for i, (src, dst) in enumerate(((k_hbm, k_buf), (v_hbm, v_buf), (w_hbm, w_buf)))
    ]
    own = []
    for sub in range(per_dest):
        for dest in range(n):
            head = dest * per_dest + sub
            own.append(
                pltpu.make_async_copy(
                    q_ref.at[0, :, pl.ds(head * HEAD_SIZE, HEAD_SIZE)],
                    q_all.at[me, sub * n + dest],
                    own_sem.at[head],
                )
            )
    for copy in own + loads:
        copy.start()

    barrier = pltpu.get_barrier_semaphore()
    for bit in range(bits):
        pl.semaphore_signal(
            barrier, inc=1, device_id={"seq": flipped(me, 1 << bit)}, device_id_type=MESH
        )
    pl.semaphore_wait(barrier, bits)

    walks = [[b for b in reversed(order) if b != 0] for order in orders]
    q_copies = []

    def q_copy(sub, c, held, bit):
        heads = pl.ds(sub * n + c * half_dests, half_dests)
        block = flipped(me, held)
        mask = held | (1 << bit)
        return pltpu.make_async_remote_copy(
            src_ref=q_all.at[block, heads],
            dst_ref=q_all.at[block, heads],
            send_sem=q_send.at[2 * sub + c, mask],
            recv_sem=q_recv.at[2 * sub + c, mask],
            device_id={"seq": flipped(me, 1 << bit)},
            device_id_type=MESH,
        )

    def q_forward(sub, c, held, step):
        for bit in walks[c][step:] + [0]:
            copy = q_copy(sub, c, held, bit)
            copy.start()
            q_copies.append(copy)

    def q_arrival(sub, c, mask):
        heads = pl.ds(sub * n + c * half_dests, half_dests)
        block = flipped(me, mask)
        pltpu.make_async_remote_copy(
            src_ref=q_all.at[block, heads],
            dst_ref=q_all.at[block, heads],
            send_sem=q_send.at[2 * sub + c, mask],
            recv_sem=q_recv.at[2 * sub + c, mask],
            device_id={"seq": flipped(me, 1)},
            device_id_type=MESH,
        ).wait_recv()

    def held_before(c, step):
        masks = [0]
        for bit in walks[c][:step]:
            masks = masks + [mask | (1 << bit) for mask in masks]
        return masks

    def q_turn(sub, step):
        for c in range(2):
            for held in held_before(c, step):
                mask = held | (1 << walks[c][step])
                q_arrival(sub, c, mask)
                q_forward(sub, c, mask, step + 1)

    def q_finish(sub):
        for c in range(2):
            for held in held_before(c, bits - 1):
                q_arrival(sub, c, held | 1)

    for copy in own:
        copy.wait()
    for c in range(2):
        q_forward(0, c, 0, 0)
    for step in range(bits - 2):
        q_turn(0, step)
        for sub in range(1, per_dest):
            if step == 0:
                for c in range(2):
                    q_forward(sub, c, 0, 0)
            else:
                q_turn(sub, step - 1)
    q_turn(0, bits - 2)
    for sub in range(1, per_dest):
        q_turn(sub, bits - 3)
    loads[0].wait()
    loads[1].wait()

    slot = lax.broadcasted_iota(jnp.int32, (key_count, rows), 0)
    row = lax.broadcasted_iota(jnp.int32, (key_count, rows), 1)
    allowed = (slot < live_ref[0]) & (me * key_count + slot <= first_ref[0] + row)

    def attend(sub, i, start):
        dest = dest_at(start + i, orders[0])
        head = dest * per_dest + sub
        key_head = head // group_width
        q = q_all[:, sub * n + dest].reshape(rows, HEAD_SIZE)
        kv_cols = pl.ds(pl.multiple_of(key_head * HEAD_SIZE, HEAD_SIZE), HEAD_SIZE)
        scores = lax.dot_general(
            k_buf[:, kv_cols], q, (((1,), (1,)), ((), ())), preferred_element_type=jnp.float32
        ) * score_scale
        scores = jnp.where(allowed, scores, masked_value)
        best = jnp.max(scores, axis=0, keepdims=True)
        weights = jnp.where(allowed, jnp.exp(scores - best), 0.0)
        total = jnp.sum(weights, axis=0, keepdims=True)
        safe = jnp.where(total > 0, total, 1.0)
        weighted = lax.dot_general(
            v_buf[:, kv_cols], weights.astype(jnp.bfloat16), (((0,), (0,)), ((), ())),
            preferred_element_type=jnp.float32,
        )
        partial = (weighted * (1.0 / safe)).astype(jnp.bfloat16)
        lse = jnp.where(total > 0, best + jnp.log(safe), masked_value)
        for c in range(2):
            at = place_of(dest, orders[c])
            parts[2 * sub + c, at] = partial[:, c * half_rows:(c + 1) * half_rows]
            lses[2 * sub + c, at] = lse[:, c * half_rows:(c + 1) * half_rows]
        return start

    def spans(c, step):
        base = 0
        for earlier in range(step):
            base = base + bit_of(me, orders[c][earlier]) * (n >> (earlier + 1))
        size = n >> (step + 1)
        mine = bit_of(me, orders[c][step])
        return base + (1 - mine) * size, base + mine * size, n - 2 * size, size

    def p_copies(f, step):
        away, _, landing, size = spans(f % 2, step)
        return [
            pltpu.make_async_remote_copy(
                src_ref=source.at[f, pl.ds(away, size)],
                dst_ref=target.at[f, pl.ds(landing, size)],
                send_sem=p_send.at[f, step, i],
                recv_sem=p_recv.at[f, step, i],
                device_id={"seq": flipped(me, 1 << orders[f % 2][step])},
                device_id_type=MESH,
            )
            for i, (source, target) in enumerate(((parts, gots), (lses, gotls)))
        ]

    def merge(f, start, landing, count):
        def one(i, carry):
            at, came_at = start + i, landing + i
            left, right = lses[f, at], gotls[f, came_at]
            top = jnp.maximum(left, right)
            scale_l, scale_r = jnp.exp(left - top), jnp.exp(right - top)
            whole = scale_l + scale_r
            inverse = 1.0 / whole
            mixed = parts[f, at].astype(jnp.float32) * (scale_l * inverse) + gots[
                f, came_at
            ].astype(jnp.float32) * (scale_r * inverse)
            parts[f, at] = mixed.astype(jnp.bfloat16)
            lses[f, at] = top + jnp.log(whole)
            return carry

        lax.fori_loop(0, count, one, 0, unroll=min(count, 4))

    pending = []
    flying = {}

    def p_start(f, step):
        flying[f] = p_copies(f, step)
        for copy in flying[f]:
            copy.start()

    def p_turn(f, step):
        _, keep, landing, size = spans(f % 2, step)
        for copy in flying[f]:
            copy.wait_recv()
        pending.extend(flying[f])
        merge(f, keep, landing, size)
        if step + 1 < bits:
            p_start(f, step + 1)

    away0, keep0, _, _ = spans(0, 0)
    turned = [0] * p_flows

    def p_advance(sub, step):
        for f in (2 * sub, 2 * sub + 1):
            if turned[f] == step:
                p_turn(f, step)
                turned[f] += 1

    for sub in range(per_dest):
        q_finish(sub)
        lax.fori_loop(0, n // 2, functools.partial(attend, sub), away0, unroll=4)
        p_start(2 * sub, 0)
        p_start(2 * sub + 1, 0)
        if sub + 1 < per_dest:
            q_turn(sub + 1, bits - 2)
        if sub > 0:
            p_advance(sub - 1, 0)
        lax.fori_loop(0, n // 2, functools.partial(attend, sub), keep0, unroll=4)
    for wave in range(bits + per_dest - 1):
        for sub in range(per_dest):
            if 0 <= wave - sub < bits:
                p_advance(sub, wave - sub)

    loads[2].wait()
    merged = []
    for c in range(2):
        at = place_of(me, orders[c])
        merged.append(
            jnp.concatenate([parts[2 * sub + c, at] for sub in range(per_dest)], axis=0)
        )

    def t_copy(f, step):
        away, _, landing, size = spans(f % 2, step)
        return pltpu.make_async_remote_copy(
            src_ref=sent.at[f, pl.ds(away, size)],
            dst_ref=came.at[f, pl.ds(landing, size)],
            send_sem=t_send.at[f, step],
            recv_sem=t_recv.at[f, step],
            device_id={"seq": flipped(me, 1 << orders[f % 2][step])},
            device_id_type=MESH,
        )

    def ship(f, step):
        away, _, _, size = spans(f % 2, step)

        def one(i, carry):
            sent[f, away + i] = acc[f, away + i].astype(jnp.bfloat16)
            return carry

        lax.fori_loop(0, size, one, 0, unroll=min(size, 4))
        copy = t_copy(f, step)
        copy.start()
        return copy

    flying = []
    for f in range(t_flows):
        for r in range(2):
            term = lax.dot_general(
                merged[r], w_buf[:, f * out_part:(f + 1) * out_part], (((0,), (0,)), ((), ())),
                preferred_element_type=jnp.float32,
            )
            for j in range(n // 2):
                at = place_of(r * (n // 2) + j, orders[f % 2])
                acc[f, at] = term[j * rows_each:(j + 1) * rows_each]
        flying.append(ship(f, 0))
    for step in range(bits):
        for f in range(t_flows):
            _, keep, landing, size = spans(f % 2, step)
            flying[f].wait_recv()
            pending.append(flying[f])

            def add(i, carry):
                acc[f, keep + i] = acc[f, keep + i] + came[f, landing + i].astype(jnp.float32)
                return carry

            lax.fori_loop(0, size, add, 0, unroll=min(size, 4))
            if step + 1 < bits:
                flying[f] = ship(f, step + 1)
    for f in range(t_flows):
        at = place_of(me, orders[f % 2])
        out_ref[:, f * out_part:(f + 1) * out_part] = acc[f, at].astype(jnp.bfloat16)
    for copy in q_copies + pending:
        copy.wait_send()


def body(query_block, cache_keys, stored_values, live_counts, first_position, out_weight):
    n = lax.axis_size("seq")
    bits = n.bit_length() - 1
    rows_each = query_block.shape[0]
    half_rows = rows_each * n // 2
    d_model = out_weight.shape[1]
    per_dest = QUERY_HEADS // n
    p_flows = 2 * per_dest
    t_flows = max(f for f in (2, 4, 6) if d_model % (128 * f) == 0)
    vmem = pl.BlockSpec(memory_space=pltpu.VMEM)
    smem = pl.BlockSpec(memory_space=pltpu.SMEM)
    anywhere = pl.BlockSpec(memory_space=pl.ANY)
    bf16, f32 = jnp.bfloat16, jnp.float32
    dma = pltpu.SemaphoreType.DMA
    return pl.pallas_call(
        functools.partial(kernel, n),
        out_shape=jax.ShapeDtypeStruct((rows_each, d_model), bf16),
        in_specs=[anywhere, smem, smem, anywhere, anywhere, anywhere],
        out_specs=vmem,
        scratch_shapes=[
            pltpu.VMEM((n, QUERY_HEADS, rows_each, HEAD_SIZE), bf16),
            pltpu.VMEM(cache_keys.shape, bf16),
            pltpu.VMEM(stored_values.shape, bf16),
            pltpu.VMEM(out_weight.shape, bf16),
            pltpu.VMEM((p_flows, n, HEAD_SIZE, half_rows), bf16),
            pltpu.VMEM((p_flows, n, 1, half_rows), f32),
            pltpu.VMEM((p_flows, n, HEAD_SIZE, half_rows), bf16),
            pltpu.VMEM((p_flows, n, 1, half_rows), f32),
            pltpu.VMEM((t_flows, n, rows_each, d_model // t_flows), f32),
            pltpu.VMEM((t_flows, n, rows_each, d_model // t_flows), bf16),
            pltpu.VMEM((t_flows, n, rows_each, d_model // t_flows), bf16),
            dma((3,)),
            dma((QUERY_HEADS,)),
            dma((p_flows, n)),
            dma((p_flows, n)),
            dma((p_flows, bits, 2)),
            dma((p_flows, bits, 2)),
            dma((t_flows, bits)),
            dma((t_flows, bits)),
        ],
        compiler_params=pltpu.CompilerParams(
            collective_id=0, has_side_effects=True, vmem_limit_bytes=63 * 1024 * 1024
        ),
        name="attend_project",
    )(query_block[None], live_counts, first_position, cache_keys, stored_values, out_weight)


def solution(mesh):
    in_specs = (
        P(("groups", "seq"), None),
        P(("groups", "seq"), None),
        P(("groups", "seq"), None),
        P(("groups", "seq")),
        P("groups"),
        P("seq", None),
    )
    out_specs = P(("groups", "seq"), None)
    return jax.shard_map(body, mesh=mesh, in_specs=in_specs, out_specs=out_specs, check_vma=False)
```

```python
import functools

import jax
import jax.numpy as jnp
from jax import lax
from jax.experimental import pallas as pl
from jax.experimental.pallas import tpu as pltpu
from jax.sharding import PartitionSpec as P

QUERY_HEADS = 32
KEY_VALUE_HEADS = 16
HEAD_SIZE = 128

score_scale = 168.0 ** (-0.5)
masked_value = -1e30
MESH = pl.DeviceIdType.MESH


def bit_of(index, bit):
    return (index // (1 << bit)) % 2


def flipped(index, mask):
    result = index
    bit = 0
    while (1 << bit) <= mask:
        if (mask >> bit) & 1:
            result = result + (1 - 2 * bit_of(index, bit)) * (1 << bit)
        bit += 1
    return result


def place_of(dest, order):
    place = 0
    for step, bit in enumerate(order):
        place = place + bit_of(dest, bit) * (1 << (len(order) - 1 - step))
    return place


def dest_at(place, order):
    dest = 0
    for step, bit in enumerate(order):
        dest = dest + bit_of(place, len(order) - 1 - step) * (1 << bit)
    return dest


def side_of(flow):
    return 1 if flow == 1 else 0


def kernel(
    n, q_ref, live_ref, first_ref, k_hbm, v_hbm, w_hbm, out_ref,
    q_all, k_buf, v_buf, w_buf, parts, lses, gots, gotls, acc, sent, came,
    load_sem, own_sem, q_send, q_recv, p_send, p_recv, t_send, t_recv,
):
    me = lax.axis_index("seq")
    bits = n.bit_length() - 1
    orders = (list(range(bits)), [0] + list(range(2, bits)) + [1])
    per_dest = QUERY_HEADS // n
    group_width = QUERY_HEADS // KEY_VALUE_HEADS
    key_count = k_buf.shape[0]
    rows_each = q_ref.shape[1]
    rows = rows_each * n
    half_rows = rows // 2
    half_dests = n // 2
    p_flows = parts.shape[0]
    t_flows, out_part = acc.shape[0], acc.shape[3]

    loads = [
        pltpu.make_async_copy(src, dst, load_sem.at[i])
        for i, (src, dst) in enumerate(((k_hbm, k_buf), (v_hbm, v_buf), (w_hbm, w_buf)))
    ]
    own = []
    for sub in range(per_dest):
        for dest in range(n):
            head = dest * per_dest + sub
            own.append(
                pltpu.make_async_copy(
                    q_ref.at[0, :, pl.ds(head * HEAD_SIZE, HEAD_SIZE)],
                    q_all.at[me, sub * n + dest],
                    own_sem.at[head],
                )
            )
    for copy in own + loads:
        copy.start()

    barrier = pltpu.get_barrier_semaphore()
    for bit in range(bits):
        pl.semaphore_signal(
            barrier, inc=1, device_id={"seq": flipped(me, 1 << bit)}, device_id_type=MESH
        )
    pl.semaphore_wait(barrier, bits)

    walks = [[b for b in reversed(order) if b != 0] for order in orders]
    q_copies = []

    def q_copy(sub, c, held, bit):
        heads = pl.ds(sub * n + c * half_dests, half_dests)
        block = flipped(me, held)
        mask = held | (1 << bit)
        return pltpu.make_async_remote_copy(
            src_ref=q_all.at[block, heads],
            dst_ref=q_all.at[block, heads],
            send_sem=q_send.at[2 * sub + c, mask],
            recv_sem=q_recv.at[2 * sub + c, mask],
            device_id={"seq": flipped(me, 1 << bit)},
            device_id_type=MESH,
        )

    def q_forward(sub, c, held, step):
        for bit in walks[side_of(2 * sub + c)][step:] + [0]:
            copy = q_copy(sub, c, held, bit)
            copy.start()
            q_copies.append(copy)

    def q_arrival(sub, c, mask):
        heads = pl.ds(sub * n + c * half_dests, half_dests)
        block = flipped(me, mask)
        pltpu.make_async_remote_copy(
            src_ref=q_all.at[block, heads],
            dst_ref=q_all.at[block, heads],
            send_sem=q_send.at[2 * sub + c, mask],
            recv_sem=q_recv.at[2 * sub + c, mask],
            device_id={"seq": flipped(me, 1)},
            device_id_type=MESH,
        ).wait_recv()

    def held_before(side, step):
        masks = [0]
        for bit in walks[side][:step]:
            masks = masks + [mask | (1 << bit) for mask in masks]
        return masks

    def q_turn(sub, step):
        for c in range(2):
            side = side_of(2 * sub + c)
            for held in held_before(side, step):
                mask = held | (1 << walks[side][step])
                q_arrival(sub, c, mask)
                q_forward(sub, c, mask, step + 1)

    def q_finish(sub):
        for c in range(2):
            for held in held_before(0, bits - 1):
                q_arrival(sub, c, held | 1)

    for copy in own:
        copy.wait()
    for c in range(2):
        q_forward(0, c, 0, 0)
    for step in range(bits - 2):
        q_turn(0, step)
        for sub in range(1, per_dest):
            if step == 0:
                for c in range(2):
                    q_forward(sub, c, 0, 0)
            else:
                q_turn(sub, step - 1)
    q_turn(0, bits - 2)
    for sub in range(1, per_dest):
        q_turn(sub, bits - 3)
    loads[0].wait()
    loads[1].wait()

    slot = lax.broadcasted_iota(jnp.int32, (key_count, rows), 0)
    row = lax.broadcasted_iota(jnp.int32, (key_count, rows), 1)
    allowed = (slot < live_ref[0]) & (me * key_count + slot <= first_ref[0] + row)

    def attend(sub, i, start):
        dest = dest_at(start + i, orders[0])
        head = dest * per_dest + sub
        key_head = head // group_width
        q = q_all[:, sub * n + dest].reshape(rows, HEAD_SIZE)
        kv_cols = pl.ds(pl.multiple_of(key_head * HEAD_SIZE, HEAD_SIZE), HEAD_SIZE)
        scores = lax.dot_general(
            k_buf[:, kv_cols], q, (((1,), (1,)), ((), ())), preferred_element_type=jnp.float32
        ) * score_scale
        scores = jnp.where(allowed, scores, masked_value)
        best = jnp.max(scores, axis=0, keepdims=True)
        weights = jnp.where(allowed, jnp.exp(scores - best), 0.0)
        total = jnp.sum(weights, axis=0, keepdims=True)
        safe = jnp.where(total > 0, total, 1.0)
        weighted = lax.dot_general(
            v_buf[:, kv_cols], weights.astype(jnp.bfloat16), (((0,), (0,)), ((), ())),
            preferred_element_type=jnp.float32,
        )
        partial = (weighted * (1.0 / safe)).astype(jnp.bfloat16)
        lse = jnp.where(total > 0, best + jnp.log(safe), masked_value)
        for c in range(2):
            at = place_of(dest, orders[side_of(2 * sub + c)])
            parts[2 * sub + c, at] = partial[:, c * half_rows:(c + 1) * half_rows]
            lses[2 * sub + c, at] = lse[:, c * half_rows:(c + 1) * half_rows]
        return start

    def spans(c, step):
        base = 0
        for earlier in range(step):
            base = base + bit_of(me, orders[c][earlier]) * (n >> (earlier + 1))
        size = n >> (step + 1)
        mine = bit_of(me, orders[c][step])
        return base + (1 - mine) * size, base + mine * size, n - 2 * size, size

    def p_copies(f, step):
        away, _, landing, size = spans(side_of(f), step)
        return [
            pltpu.make_async_remote_copy(
                src_ref=source.at[f, pl.ds(away, size)],
                dst_ref=target.at[f, pl.ds(landing, size)],
                send_sem=p_send.at[f, step, i],
                recv_sem=p_recv.at[f, step, i],
                device_id={"seq": flipped(me, 1 << orders[side_of(f)][step])},
                device_id_type=MESH,
            )
            for i, (source, target) in enumerate(((parts, gots), (lses, gotls)))
        ]

    def merge(f, start, landing, count):
        def one(i, carry):
            at, came_at = start + i, landing + i
            left, right = lses[f, at], gotls[f, came_at]
            top = jnp.maximum(left, right)
            scale_l, scale_r = jnp.exp(left - top), jnp.exp(right - top)
            whole = scale_l + scale_r
            inverse = 1.0 / whole
            mixed = parts[f, at].astype(jnp.float32) * (scale_l * inverse) + gots[
                f, came_at
            ].astype(jnp.float32) * (scale_r * inverse)
            parts[f, at] = mixed.astype(jnp.bfloat16)
            lses[f, at] = top + jnp.log(whole)
            return carry

        lax.fori_loop(0, count, one, 0, unroll=min(count, 4))

    pending = []
    flying = {}

    def p_start(f, step):
        flying[f] = p_copies(f, step)
        for copy in flying[f]:
            copy.start()

    def p_turn(f, step):
        _, keep, landing, size = spans(side_of(f), step)
        for copy in flying[f]:
            copy.wait_recv()
        pending.extend(flying[f])
        merge(f, keep, landing, size)
        if step + 1 < bits:
            p_start(f, step + 1)

    away0, keep0, _, _ = spans(0, 0)
    turned = [0] * p_flows

    def p_advance(sub, step):
        for f in (2 * sub, 2 * sub + 1):
            if turned[f] == step:
                p_turn(f, step)
                turned[f] += 1

    for sub in range(per_dest):
        q_finish(sub)
        lax.fori_loop(0, n // 2, functools.partial(attend, sub), away0, unroll=4)
        p_start(2 * sub, 0)
        p_start(2 * sub + 1, 0)
        if sub + 1 < per_dest:
            q_turn(sub + 1, bits - 2)
        if sub > 0:
            p_advance(sub - 1, 0)
        lax.fori_loop(0, n // 2, functools.partial(attend, sub), keep0, unroll=4)
    for wave in range(bits + per_dest - 1):
        for sub in range(per_dest):
            if 0 <= wave - sub < bits:
                p_advance(sub, wave - sub)

    loads[2].wait()
    merged = []
    for c in range(2):
        merged.append(
            jnp.concatenate(
                [
                    parts[f, place_of(me, orders[side_of(f)])]
                    for f in range(c, p_flows, 2)
                ],
                axis=0,
            )
        )

    def t_copy(f, step):
        away, _, landing, size = spans(side_of(f), step)
        return pltpu.make_async_remote_copy(
            src_ref=sent.at[f, pl.ds(away, size)],
            dst_ref=came.at[f, pl.ds(landing, size)],
            send_sem=t_send.at[f, step],
            recv_sem=t_recv.at[f, step],
            device_id={"seq": flipped(me, 1 << orders[side_of(f)][step])},
            device_id_type=MESH,
        )

    def ship(f, step):
        away, _, _, size = spans(side_of(f), step)

        def one(i, carry):
            sent[f, away + i] = acc[f, away + i].astype(jnp.bfloat16)
            return carry

        lax.fori_loop(0, size, one, 0, unroll=min(size, 4))
        copy = t_copy(f, step)
        copy.start()
        return copy

    flying = []
    for f in range(t_flows):
        for r in range(2):
            term = lax.dot_general(
                merged[r], w_buf[:, f * out_part:(f + 1) * out_part], (((0,), (0,)), ((), ())),
                preferred_element_type=jnp.float32,
            )
            for j in range(n // 2):
                at = place_of(r * (n // 2) + j, orders[side_of(f)])
                acc[f, at] = term[j * rows_each:(j + 1) * rows_each]
        flying.append(ship(f, 0))
    for step in range(bits):
        for f in range(t_flows):
            _, keep, landing, size = spans(side_of(f), step)
            flying[f].wait_recv()
            pending.append(flying[f])

            def add(i, carry):
                acc[f, keep + i] = acc[f, keep + i] + came[f, landing + i].astype(jnp.float32)
                return carry

            lax.fori_loop(0, size, add, 0, unroll=min(size, 4))
            if step + 1 < bits:
                flying[f] = ship(f, step + 1)
    for f in range(t_flows):
        at = place_of(me, orders[side_of(f)])
        out_ref[:, f * out_part:(f + 1) * out_part] = acc[f, at].astype(jnp.bfloat16)
    for copy in q_copies + pending:
        copy.wait_send()


def body(query_block, cache_keys, stored_values, live_counts, first_position, out_weight):
    n = lax.axis_size("seq")
    bits = n.bit_length() - 1
    rows_each = query_block.shape[0]
    half_rows = rows_each * n // 2
    d_model = out_weight.shape[1]
    per_dest = QUERY_HEADS // n
    p_flows = 2 * per_dest
    t_flows = max(f for f in (2, 4, 6) if d_model % (128 * f) == 0)
    vmem = pl.BlockSpec(memory_space=pltpu.VMEM)
    smem = pl.BlockSpec(memory_space=pltpu.SMEM)
    anywhere = pl.BlockSpec(memory_space=pl.ANY)
    bf16, f32 = jnp.bfloat16, jnp.float32
    dma = pltpu.SemaphoreType.DMA
    return pl.pallas_call(
        functools.partial(kernel, n),
        out_shape=jax.ShapeDtypeStruct((rows_each, d_model), bf16),
        in_specs=[anywhere, smem, smem, anywhere, anywhere, anywhere],
        out_specs=vmem,
        scratch_shapes=[
            pltpu.VMEM((n, QUERY_HEADS, rows_each, HEAD_SIZE), bf16),
            pltpu.VMEM(cache_keys.shape, bf16),
            pltpu.VMEM(stored_values.shape, bf16),
            pltpu.VMEM(out_weight.shape, bf16),
            pltpu.VMEM((p_flows, n, HEAD_SIZE, half_rows), bf16),
            pltpu.VMEM((p_flows, n, 1, half_rows), f32),
            pltpu.VMEM((p_flows, n, HEAD_SIZE, half_rows), bf16),
            pltpu.VMEM((p_flows, n, 1, half_rows), f32),
            pltpu.VMEM((t_flows, n, rows_each, d_model // t_flows), f32),
            pltpu.VMEM((t_flows, n, rows_each, d_model // t_flows), bf16),
            pltpu.VMEM((t_flows, n, rows_each, d_model // t_flows), bf16),
            dma((3,)),
            dma((QUERY_HEADS,)),
            dma((p_flows, n)),
            dma((p_flows, n)),
            dma((p_flows, bits, 2)),
            dma((p_flows, bits, 2)),
            dma((t_flows, bits)),
            dma((t_flows, bits)),
        ],
        compiler_params=pltpu.CompilerParams(
            collective_id=0, has_side_effects=True, vmem_limit_bytes=63 * 1024 * 1024
        ),
        name="attend_project",
    )(query_block[None], live_counts, first_position, cache_keys, stored_values, out_weight)


def solution(mesh):
    in_specs = (
        P(("groups", "seq"), None),
        P(("groups", "seq"), None),
        P(("groups", "seq"), None),
        P(("groups", "seq")),
        P("groups"),
        P("seq", None),
    )
    out_specs = P(("groups", "seq"), None)
    return jax.shard_map(body, mesh=mesh, in_specs=in_specs, out_specs=out_specs, check_vma=False)
```

```python
import functools

import jax
import jax.numpy as jnp
from jax import lax
from jax.experimental import pallas as pl
from jax.experimental.pallas import tpu as pltpu
from jax.sharding import PartitionSpec as P

QUERY_HEADS = 32
KEY_VALUE_HEADS = 16
HEAD_SIZE = 128

score_scale = 168.0 ** (-0.5)
masked_value = -1e30
MESH = pl.DeviceIdType.MESH


def bit_of(index, bit):
    return (index // (1 << bit)) % 2


def flipped(index, mask):
    result = index
    bit = 0
    while (1 << bit) <= mask:
        if (mask >> bit) & 1:
            result = result + (1 - 2 * bit_of(index, bit)) * (1 << bit)
        bit += 1
    return result


def place_of(dest, order):
    place = 0
    for step, bit in enumerate(order):
        place = place + bit_of(dest, bit) * (1 << (len(order) - 1 - step))
    return place


def dest_at(place, order):
    dest = 0
    for step, bit in enumerate(order):
        dest = dest + bit_of(place, len(order) - 1 - step) * (1 << bit)
    return dest


def side_of(flow):
    return 1 if flow in (1, 4) else 0


def kernel(
    n, q_ref, live_ref, first_ref, k_hbm, v_hbm, w_hbm, out_ref,
    q_all, k_buf, v_buf, w_buf, parts, lses, gots, gotls, acc, sent, came,
    load_sem, own_sem, q_send, q_recv, p_send, p_recv, t_send, t_recv,
):
    me = lax.axis_index("seq")
    bits = n.bit_length() - 1
    orders = (list(range(bits)), [0] + list(range(2, bits)) + [1])
    per_dest = QUERY_HEADS // n
    group_width = QUERY_HEADS // KEY_VALUE_HEADS
    key_count = k_buf.shape[0]
    rows_each = q_ref.shape[1]
    rows = rows_each * n
    half_rows = rows // 2
    half_dests = n // 2
    p_flows = parts.shape[0]
    t_flows, out_part = acc.shape[0], acc.shape[3]

    loads = [
        pltpu.make_async_copy(src, dst, load_sem.at[i])
        for i, (src, dst) in enumerate(((k_hbm, k_buf), (v_hbm, v_buf), (w_hbm, w_buf)))
    ]
    own = []
    for sub in range(per_dest):
        for dest in range(n):
            head = dest * per_dest + sub
            own.append(
                pltpu.make_async_copy(
                    q_ref.at[0, :, pl.ds(head * HEAD_SIZE, HEAD_SIZE)],
                    q_all.at[me, sub * n + dest],
                    own_sem.at[head],
                )
            )
    for copy in own + loads:
        copy.start()

    barrier = pltpu.get_barrier_semaphore()
    for bit in range(bits):
        pl.semaphore_signal(
            barrier, inc=1, device_id={"seq": flipped(me, 1 << bit)}, device_id_type=MESH
        )
    pl.semaphore_wait(barrier, bits)

    walks = [[b for b in reversed(order) if b != 0] for order in orders]
    q_copies = []

    def q_copy(sub, c, held, bit):
        heads = pl.ds(sub * n + c * half_dests, half_dests)
        block = flipped(me, held)
        mask = held | (1 << bit)
        return pltpu.make_async_remote_copy(
            src_ref=q_all.at[block, heads],
            dst_ref=q_all.at[block, heads],
            send_sem=q_send.at[2 * sub + c, mask],
            recv_sem=q_recv.at[2 * sub + c, mask],
            device_id={"seq": flipped(me, 1 << bit)},
            device_id_type=MESH,
        )

    def q_forward(sub, c, held, step):
        for bit in walks[side_of(2 * sub + c)][step:] + [0]:
            copy = q_copy(sub, c, held, bit)
            copy.start()
            q_copies.append(copy)

    def q_arrival(sub, c, mask):
        heads = pl.ds(sub * n + c * half_dests, half_dests)
        block = flipped(me, mask)
        pltpu.make_async_remote_copy(
            src_ref=q_all.at[block, heads],
            dst_ref=q_all.at[block, heads],
            send_sem=q_send.at[2 * sub + c, mask],
            recv_sem=q_recv.at[2 * sub + c, mask],
            device_id={"seq": flipped(me, 1)},
            device_id_type=MESH,
        ).wait_recv()

    def held_before(side, step):
        masks = [0]
        for bit in walks[side][:step]:
            masks = masks + [mask | (1 << bit) for mask in masks]
        return masks

    def q_turn(sub, step):
        for c in range(2):
            side = side_of(2 * sub + c)
            for held in held_before(side, step):
                mask = held | (1 << walks[side][step])
                q_arrival(sub, c, mask)
                q_forward(sub, c, mask, step + 1)

    def q_finish(sub):
        for c in range(2):
            for held in held_before(0, bits - 1):
                q_arrival(sub, c, held | 1)

    for copy in own:
        copy.wait()
    for c in range(2):
        q_forward(0, c, 0, 0)
    for step in range(bits - 2):
        q_turn(0, step)
        for sub in range(1, per_dest):
            if step == 0:
                for c in range(2):
                    q_forward(sub, c, 0, 0)
            else:
                q_turn(sub, step - 1)
    q_turn(0, bits - 2)
    for sub in range(1, per_dest):
        q_turn(sub, bits - 3)
    loads[0].wait()
    loads[1].wait()

    slot = lax.broadcasted_iota(jnp.int32, (key_count, rows), 0)
    row = lax.broadcasted_iota(jnp.int32, (key_count, rows), 1)
    allowed = (slot < live_ref[0]) & (me * key_count + slot <= first_ref[0] + row)

    def attend(sub, i, start):
        dest = dest_at(start + i, orders[0])
        head = dest * per_dest + sub
        key_head = head // group_width
        q = q_all[:, sub * n + dest].reshape(rows, HEAD_SIZE)
        kv_cols = pl.ds(pl.multiple_of(key_head * HEAD_SIZE, HEAD_SIZE), HEAD_SIZE)
        scores = lax.dot_general(
            k_buf[:, kv_cols], q, (((1,), (1,)), ((), ())), preferred_element_type=jnp.float32
        ) * score_scale
        scores = jnp.where(allowed, scores, masked_value)
        best = jnp.max(scores, axis=0, keepdims=True)
        weights = jnp.where(allowed, jnp.exp(scores - best), 0.0)
        total = jnp.sum(weights, axis=0, keepdims=True)
        safe = jnp.where(total > 0, total, 1.0)
        weighted = lax.dot_general(
            v_buf[:, kv_cols], weights.astype(jnp.bfloat16), (((0,), (0,)), ((), ())),
            preferred_element_type=jnp.float32,
        )
        partial = (weighted * (1.0 / safe)).astype(jnp.bfloat16)
        lse = jnp.where(total > 0, best + jnp.log(safe), masked_value)
        for c in range(2):
            at = place_of(dest, orders[side_of(2 * sub + c)])
            parts[2 * sub + c, at] = partial[:, c * half_rows:(c + 1) * half_rows]
            lses[2 * sub + c, at] = lse[:, c * half_rows:(c + 1) * half_rows]
        return start

    def spans(c, step):
        base = 0
        for earlier in range(step):
            base = base + bit_of(me, orders[c][earlier]) * (n >> (earlier + 1))
        size = n >> (step + 1)
        mine = bit_of(me, orders[c][step])
        return base + (1 - mine) * size, base + mine * size, n - 2 * size, size

    def p_copies(f, step):
        away, _, landing, size = spans(side_of(f), step)
        return [
            pltpu.make_async_remote_copy(
                src_ref=source.at[f, pl.ds(away, size)],
                dst_ref=target.at[f, pl.ds(landing, size)],
                send_sem=p_send.at[f, step, i],
                recv_sem=p_recv.at[f, step, i],
                device_id={"seq": flipped(me, 1 << orders[side_of(f)][step])},
                device_id_type=MESH,
            )
            for i, (source, target) in enumerate(((parts, gots), (lses, gotls)))
        ]

    def merge(f, start, landing, count):
        def one(i, carry):
            at, came_at = start + i, landing + i
            left, right = lses[f, at], gotls[f, came_at]
            top = jnp.maximum(left, right)
            scale_l, scale_r = jnp.exp(left - top), jnp.exp(right - top)
            whole = scale_l + scale_r
            inverse = 1.0 / whole
            mixed = parts[f, at].astype(jnp.float32) * (scale_l * inverse) + gots[
                f, came_at
            ].astype(jnp.float32) * (scale_r * inverse)
            parts[f, at] = mixed.astype(jnp.bfloat16)
            lses[f, at] = top + jnp.log(whole)
            return carry

        lax.fori_loop(0, count, one, 0, unroll=min(count, 4))

    pending = []
    flying = {}

    def p_start(f, step):
        flying[f] = p_copies(f, step)
        for copy in flying[f]:
            copy.start()

    def p_turn(f, step):
        _, keep, landing, size = spans(side_of(f), step)
        for copy in flying[f]:
            copy.wait_recv()
        pending.extend(flying[f])
        merge(f, keep, landing, size)
        if step + 1 < bits:
            p_start(f, step + 1)

    away0, keep0, _, _ = spans(0, 0)
    turned = [0] * p_flows

    def p_advance(sub, step):
        for f in (2 * sub, 2 * sub + 1):
            if turned[f] == step:
                p_turn(f, step)
                turned[f] += 1

    for sub in range(per_dest):
        q_finish(sub)
        lax.fori_loop(0, n // 2, functools.partial(attend, sub), away0, unroll=4)
        p_start(2 * sub, 0)
        p_start(2 * sub + 1, 0)
        if sub + 1 < per_dest:
            q_turn(sub + 1, bits - 2)
        if sub > 0:
            p_advance(sub - 1, 0)
        lax.fori_loop(0, n // 2, functools.partial(attend, sub), keep0, unroll=4)
    for wave in range(bits + per_dest - 1):
        for sub in range(per_dest):
            if 0 <= wave - sub < bits:
                p_advance(sub, wave - sub)

    loads[2].wait()
    merged = []
    for c in range(2):
        merged.append(
            jnp.concatenate(
                [
                    parts[f, place_of(me, orders[side_of(f)])]
                    for f in range(c, p_flows, 2)
                ],
                axis=0,
            )
        )

    def t_copy(f, step):
        away, _, landing, size = spans(side_of(f), step)
        return pltpu.make_async_remote_copy(
            src_ref=sent.at[f, pl.ds(away, size)],
            dst_ref=came.at[f, pl.ds(landing, size)],
            send_sem=t_send.at[f, step],
            recv_sem=t_recv.at[f, step],
            device_id={"seq": flipped(me, 1 << orders[side_of(f)][step])},
            device_id_type=MESH,
        )

    def ship(f, step):
        away, _, _, size = spans(side_of(f), step)

        def one(i, carry):
            sent[f, away + i] = acc[f, away + i].astype(jnp.bfloat16)
            return carry

        lax.fori_loop(0, size, one, 0, unroll=min(size, 4))
        copy = t_copy(f, step)
        copy.start()
        return copy

    flying = []
    for f in range(t_flows):
        for r in range(2):
            term = lax.dot_general(
                merged[r], w_buf[:, f * out_part:(f + 1) * out_part], (((0,), (0,)), ((), ())),
                preferred_element_type=jnp.float32,
            )
            for j in range(n // 2):
                at = place_of(r * (n // 2) + j, orders[side_of(f)])
                acc[f, at] = term[j * rows_each:(j + 1) * rows_each]
        flying.append(ship(f, 0))
    for step in range(bits):
        for f in range(t_flows):
            _, keep, landing, size = spans(side_of(f), step)
            flying[f].wait_recv()
            pending.append(flying[f])

            def add(i, carry):
                acc[f, keep + i] = acc[f, keep + i] + came[f, landing + i].astype(jnp.float32)
                return carry

            lax.fori_loop(0, size, add, 0, unroll=min(size, 4))
            if step + 1 < bits:
                flying[f] = ship(f, step + 1)
    for f in range(t_flows):
        at = place_of(me, orders[side_of(f)])
        out_ref[:, f * out_part:(f + 1) * out_part] = acc[f, at].astype(jnp.bfloat16)
    for copy in q_copies + pending:
        copy.wait_send()


def body(query_block, cache_keys, stored_values, live_counts, first_position, out_weight):
    n = lax.axis_size("seq")
    bits = n.bit_length() - 1
    rows_each = query_block.shape[0]
    half_rows = rows_each * n // 2
    d_model = out_weight.shape[1]
    per_dest = QUERY_HEADS // n
    p_flows = 2 * per_dest
    t_flows = max(f for f in (2, 4, 6) if d_model % (128 * f) == 0)
    vmem = pl.BlockSpec(memory_space=pltpu.VMEM)
    smem = pl.BlockSpec(memory_space=pltpu.SMEM)
    anywhere = pl.BlockSpec(memory_space=pl.ANY)
    bf16, f32 = jnp.bfloat16, jnp.float32
    dma = pltpu.SemaphoreType.DMA
    return pl.pallas_call(
        functools.partial(kernel, n),
        out_shape=jax.ShapeDtypeStruct((rows_each, d_model), bf16),
        in_specs=[anywhere, smem, smem, anywhere, anywhere, anywhere],
        out_specs=vmem,
        scratch_shapes=[
            pltpu.VMEM((n, QUERY_HEADS, rows_each, HEAD_SIZE), bf16),
            pltpu.VMEM(cache_keys.shape, bf16),
            pltpu.VMEM(stored_values.shape, bf16),
            pltpu.VMEM(out_weight.shape, bf16),
            pltpu.VMEM((p_flows, n, HEAD_SIZE, half_rows), bf16),
            pltpu.VMEM((p_flows, n, 1, half_rows), f32),
            pltpu.VMEM((p_flows, n, HEAD_SIZE, half_rows), bf16),
            pltpu.VMEM((p_flows, n, 1, half_rows), f32),
            pltpu.VMEM((t_flows, n, rows_each, d_model // t_flows), f32),
            pltpu.VMEM((t_flows, n, rows_each, d_model // t_flows), bf16),
            pltpu.VMEM((t_flows, n, rows_each, d_model // t_flows), bf16),
            dma((3,)),
            dma((QUERY_HEADS,)),
            dma((p_flows, n)),
            dma((p_flows, n)),
            dma((p_flows, bits, 2)),
            dma((p_flows, bits, 2)),
            dma((t_flows, bits)),
            dma((t_flows, bits)),
        ],
        compiler_params=pltpu.CompilerParams(
            collective_id=0, has_side_effects=True, vmem_limit_bytes=63 * 1024 * 1024
        ),
        name="attend_project",
    )(query_block[None], live_counts, first_position, cache_keys, stored_values, out_weight)


def solution(mesh):
    in_specs = (
        P(("groups", "seq"), None),
        P(("groups", "seq"), None),
        P(("groups", "seq"), None),
        P(("groups", "seq")),
        P("groups"),
        P("seq", None),
    )
    out_specs = P(("groups", "seq"), None)
    return jax.shard_map(body, mesh=mesh, in_specs=in_specs, out_specs=out_specs, check_vma=False)
```
